128 devices in a mesh: dp: 16 (over x_lo, z, core), seq: 8 (over x_hi, y).
Axes of the slice: x: 4 (x_hi: 2, x_lo: 2; x = x_hi * 2 + x_lo), y: 4, z: 4, core: 2. Of those that a mesh axis runs over, the one named last changes fastest.
Arguments:
- queries: bfloat16 [16, 2048, 64, 128], P('dp', 'seq')
- keys: bfloat16 [16, 2048, 8, 128], P('dp', 'seq')
- values: bfloat16 [16, 2048, 8, 128], P('dp', 'seq'), may hold values from -6 to 6
- doc_lengths: int32 [16, 16], replicated, may hold values from 1 to 2033, as said below
Outputs:
- attended: bfloat16 [16, 2048, 64, 128], P('dp', 'seq')
The draws below stay inside these ranges and needn't reach their ends.
Inputs may be any that keep to these rules, and one draw needn't show every extreme that they name: `doc_lengths`: each row sums to 2048; of the sequences s and s + 8, one holds a document of more than 1024 tokens; the least and the most are reached in every draw.
All inputs are finite; a program needn't handle non-finite values.
Results may differ from the reference program's by a relative error of at most 0.003.
Values may be sent and summed in bfloat16 or wider, within the bound.
A program may use at most 192 MiB of HBM per device.

```python
import jax
import jax.numpy as jnp
from jax import lax

QUERY_HEADS = 64
KEY_VALUE_HEADS = 8
HEAD_SIZE = 128
DOCS = 16
PACKED_LENGTH = 2048
PACKED_COUNT = 16


def paired_fields(key):
    key_q = jax.random.fold_in(key, 11)
    key_random_split = jax.random.fold_in(key, 12)
    queries = jnp.clip(jax.random.normal(key_q, (PACKED_COUNT, PACKED_LENGTH, QUERY_HEADS, HEAD_SIZE), jnp.float32), -6.0, 6.0)
    keys = jnp.clip(jax.random.normal(key_random_split, (PACKED_COUNT, PACKED_LENGTH, KEY_VALUE_HEADS, HEAD_SIZE), jnp.float32), -6.0, 6.0)
    return (queries, keys)


def draw_queries(key, part):
    return paired_fields(key)[0].astype(jnp.bfloat16)


def draw_keys(key, part):
    return paired_fields(key)[1].astype(jnp.bfloat16)


def draw_doc_lengths(key, part):
    base = PACKED_LENGTH // DOCS
    jitter = jax.random.randint(jax.random.fold_in(key, 21), (PACKED_COUNT, DOCS), 0, base // 2)
    light = base + jitter - jnp.roll(jitter, 1, axis=1)
    small = jax.random.randint(jax.random.fold_in(key, 22), (PACKED_COUNT, DOCS), 1, 5)
    row_index = jnp.arange(PACKED_COUNT, dtype=jnp.int32)
    first_pair = (row_index == 0) | (row_index == PACKED_COUNT // 2)
    small = jnp.where(first_pair[:, None], 1, small)
    first = PACKED_LENGTH - jnp.sum(small[:, 1:], axis=1)
    heavy = small.at[:, 0].set(first)
    coins = jax.random.randint(jax.random.fold_in(key, 23), (PACKED_COUNT // 2,), 0, 2)
    heavy_rows = jnp.concatenate([coins == 1, coins == 0])
    return jnp.where(heavy_rows[:, None], heavy, light).astype(jnp.int32)


def block_scale(own_key, shape, shards, smallest, largest):
    def one(position, blocks):
        steps = jax.random.uniform(jax.random.fold_in(jax.random.fold_in(own_key, 6), position), (blocks,), jnp.float32, smallest / len(shards), largest / len(shards))
        return jnp.repeat(jnp.exp(steps), shape[position] // blocks).reshape((-1,) + (1,) * (len(shape) - position - 1))

    gain = one(*shards[0])
    for cut in shards[1:]:
        gain = gain * one(*cut)
    return gain


def gaussian(key, shape, scale, most, pieces=(), kind=jnp.bfloat16):
    loudness = block_scale(key, shape, pieces, -0.22, 0.18) if pieces else 1.0
    values = jax.random.normal(key, shape, jnp.float32) * scale * loudness
    return jnp.minimum(jnp.maximum(values, -most), most).astype(kind)


def setup_inputs(seed: int = 0) -> dict:
    key_of = jax.random.split(jax.random.key(seed), 5)
    return {
        "queries": draw_queries(jax.random.fold_in(key_of[4], 71), 0),
        "keys": draw_keys(jax.random.fold_in(key_of[4], 71), 0),
        "values": gaussian(key_of[2], (PACKED_COUNT, PACKED_LENGTH, KEY_VALUE_HEADS, HEAD_SIZE), 1.0, 6.0, ((0, 16), (1, 8))),
        "doc_lengths": draw_doc_lengths(jax.random.fold_in(key_of[4], 71), 0),
    }


def segments_of(lengths, count):
    ends = jnp.cumsum(lengths)
    places = jnp.arange(count, dtype=jnp.int32)
    return jnp.sum((ends[None, :] <= places[:, None]).astype(jnp.int32), axis=1)


def reference(queries, keys, values, doc_lengths):
    group_size = QUERY_HEADS // KEY_VALUE_HEADS
    scale = HEAD_SIZE ** -0.5

    def one_sequence(items):
        query_rows, ks, vs, lens = items
        seg = segments_of(lens, PACKED_LENGTH)
        places = jnp.arange(PACKED_LENGTH, dtype=jnp.int32)
        allowed = (places[None, :] <= places[:, None]) & (seg[None, :] == seg[:, None])
        query_grouped = query_rows.reshape(PACKED_LENGTH, KEY_VALUE_HEADS, group_size, HEAD_SIZE).transpose(1, 0, 2, 3)
        k_heads = ks.transpose(1, 0, 2)
        v_heads = vs.transpose(1, 0, 2)

        def one_head(parts):
            qg, kh, vh = parts
            scores = jnp.einsum("qgd,kd->gqk", qg.astype(jnp.float32), kh.astype(jnp.float32)) * scale
            scores = jnp.where(allowed[None], scores, -1e30)
            peak = jnp.max(scores, axis=-1, keepdims=True)
            expo = jnp.where(allowed[None], jnp.exp(scores - peak), 0.0)
            total = jnp.sum(expo, axis=-1)
            weights = lax.optimization_barrier(expo.astype(jnp.bfloat16)).astype(jnp.float32)
            summed = jnp.einsum("gqk,kd->qgd", weights, vh.astype(jnp.float32))
            return (summed / total.T[:, :, None]).astype(jnp.bfloat16)

        heads_out = lax.map(one_head, (query_grouped, k_heads, v_heads))
        return heads_out.transpose(1, 0, 2, 3).reshape(PACKED_LENGTH, QUERY_HEADS, HEAD_SIZE)

    return lax.map(one_sequence, (queries, keys, values, doc_lengths))
```

```python
import functools

import jax
import jax.numpy as jnp
from jax import lax
from jax.experimental import pallas as pl
from jax.experimental.pallas import tpu as pltpu
from jax.sharding import PartitionSpec as P

MESH = pl.DeviceIdType.MESH
LOG2E = 1.4426950408889634
BIG = float(2.0**120)
AHEAD = 2


def attention(docs, lens, q_hbm, k_hbm, v_hbm, o_hbm, qv, raw, wide, kv, ov, q_mark, k_mark,
              send_sem, recv_sem, in_sem, out_sem):
    groups, shards, _, rows, width = kv.shape
    per_group = qv.shape[2]
    half = shards // 2
    dp = lax.axis_index("dp")
    me = lax.axis_index("seq")
    hi = me // half
    y = me % half
    upper = hi == 1
    lower = hi == 0
    right = (y + 1) % half
    left = (y + half - 1) % half

    def q_copy(g):
        return pltpu.make_async_copy(
            q_hbm.at[:, pl.ds(pl.multiple_of(g * per_group, per_group), per_group), :], qv.at[g], in_sem.at[2 + g]
        )

    def o_copy(g):
        return pltpu.make_async_copy(
            ov.at[g], o_hbm.at[:, pl.ds(pl.multiple_of(g * per_group, per_group), per_group), :], out_sem.at[g]
        )

    k_in = pltpu.make_async_copy(k_hbm, raw.at[0], in_sem.at[0])
    v_in = pltpu.make_async_copy(v_hbm, raw.at[1], in_sem.at[1])
    k_in.start()
    v_in.start()
    for g in range(groups):
        q_copy(g).start()

    barrier = pltpu.get_barrier_semaphore()
    for step in range(1, shards):
        pl.semaphore_signal(barrier, inc=1, device_id=(dp, (me + step) % shards), device_id_type=MESH)

    for which, copy in ((0, k_in), (1, v_in)):
        copy.wait()
        wide[...] = raw[which].astype(jnp.float32).reshape(rows * groups, width)
        for g in range(groups):
            kv[g, me, which] = wide[pl.ds(g, rows, stride=groups), :].astype(jnp.bfloat16)

    lane = lax.broadcasted_iota(jnp.int32, (1, width), 1)
    begin = jnp.zeros((1, width), jnp.int32)
    end = jnp.zeros((1, width), jnp.int32)
    so_far = jnp.int32(0)
    for j in range(docs):
        begin = jnp.where(lane == j, so_far, begin)
        so_far = so_far + lens[dp, j]
        end = jnp.where(lane == j, so_far, end)
    for s in range(shards):
        place = s * rows + lax.broadcasted_iota(jnp.int32, (rows, width), 0)
        inside = (place >= begin) & (place < end)
        k_mark[s] = jnp.where(inside, 1.0, 0.0).astype(jnp.bfloat16)
    k_mark[shards] = jnp.where(lax.broadcasted_iota(jnp.int32, (rows, width), 1) == docs, 1.0, 0.0).astype(jnp.bfloat16)
    place = me * rows + lax.broadcasted_iota(jnp.int32, (rows * per_group, width), 0) // per_group
    inside = ((place >= begin) & (place < end)) | (lane > docs)
    q_mark[...] = jnp.where(inside, 0.0, -BIG).astype(jnp.bfloat16)

    pl.semaphore_wait(barrier, shards - 1)

    def remote(g, shard, slot, target):
        return pltpu.make_async_remote_copy(
            src_ref=kv.at[g, shard],
            dst_ref=kv.at[g, shard],
            send_sem=send_sem.at[g, slot],
            recv_sem=recv_sem.at[g, shard],
            device_id=(dp, target),
            device_id_type=MESH,
        )

    own = [
        (lower, me, 0, half + y),
        (lower, me, 1, half + right),
        (lower & (y < 3), me, 2, y + 1),
        (lower & (y < 2), me, 3, y + 2),
        (lower & (y < 1), me, 4, y + 3),
        (upper & (y < 3), me, 0, half + y + 1),
        (upper & (y == 0), me, 1, half + 3),
        (upper & (y == 1), me, 1, half + 3),
    ]
    relayed = [
        (upper, left, 5, half + right),
        (upper, y, 6, half + left),
        (upper & (y == 3), jnp.int32(half), 7, half + 2),
    ]

    def start(table, g):
        for cond, shard, slot, target in table:
            @pl.when(cond)
            def _(shard=shard, slot=slot, target=target):
                remote(g, shard, slot, target).start()

    def arrived(g, shard, cond):
        @pl.when(cond)
        def _():
            remote(g, shard, 0, (me + 1) % shards).wait_recv()

    def relay(g):
        arrived(g, y, upper)
        arrived(g, left, upper)
        arrived(g, jnp.int32(half), upper & (y == 3))
        start(relayed, g)

    def rest(g):
        for s in range(shards - 1):
            early = upper & ((s == y) | (s == left) | ((s == half) & (y == 3)))
            arrived(g, s, (s < me) & jnp.logical_not(early))

    scale = float(width) ** -0.5 * LOG2E
    tile_tokens = 64
    tile = tile_tokens * per_group
    ones = jnp.ones((rows, width), jnp.bfloat16)

    def tile_pass(g, t, pairs):
        q = qv[g, pl.ds(pl.multiple_of(t * tile_tokens, tile_tokens), tile_tokens)].reshape(tile, width)
        marks = q_mark[pl.ds(pl.multiple_of(t * tile, tile), tile), :]
        queries = jnp.concatenate([q, marks], axis=1)
        peak = summed = None
        for p in range(pairs):
            ks, vs = [], []
            for s in (2 * p, 2 * p + 1):
                if s == 0:
                    block = mark = me
                else:
                    block = jnp.where(s <= me, s - 1, me)
                    mark = jnp.where(s <= me, s - 1, shards)
                ks.append(jnp.concatenate([kv[g, block, 0], k_mark[mark]], axis=1))
                vs.append(jnp.concatenate([kv[g, block, 1], ones], axis=1))
            k = jnp.concatenate(ks, axis=0)
            v = jnp.concatenate(vs, axis=0)
            scores = lax.dot_general(queries, k, (((1,), (1,)), ((), ())), preferred_element_type=jnp.float32)
            if p == 0:
                token = t * tile_tokens + lax.broadcasted_iota(jnp.int32, (tile, rows), 0) // per_group
                column = lax.broadcasted_iota(jnp.int32, (tile, rows), 1)
                own_part = jnp.where(column <= token, scores[:, :rows], -BIG)
                scores = jnp.concatenate([own_part, scores[:, rows:]], axis=1)
            top = jnp.max(scores, axis=1, keepdims=True)
            fresh = top if peak is None else jnp.maximum(peak, top)
            weights = jnp.exp2(scores * scale - fresh * scale).astype(jnp.bfloat16)
            product = jnp.dot(weights, v, preferred_element_type=jnp.float32)
            if peak is None:
                summed = product
            else:
                summed = summed * jnp.exp2((peak - fresh) * scale) + product
            peak = fresh
        out = (summed[:, :width] / summed[:, width:]).astype(jnp.bfloat16)
        ov[g, pl.ds(pl.multiple_of(t * tile_tokens, tile_tokens), tile_tokens)] = out.reshape(
            tile_tokens, per_group, width
        )

    def compute(g):
        for pairs in range(1, shards // 2 + 1):
            @pl.when(me // 2 + 1 == pairs)
            def _(pairs=pairs):
                def body(t, _):
                    tile_pass(g, t, pairs)
                    return 0

                lax.fori_loop(0, rows // tile_tokens, body, 0)

    for g in range(AHEAD):
        start(own, g)
    relay(0)

    def head(g, _):
        @pl.when(g + AHEAD < groups)
        def _():
            start(own, g + AHEAD)

        @pl.when(g + 1 < groups)
        def _():
            relay(g + 1)

        rest(g)
        q_copy(g).wait()
        compute(g)
        o_copy(g).start()
        return 0

    lax.fori_loop(0, groups, head, 0)

    def drain(g, _):
        o_copy(g).wait()
        for cond, shard, slot, target in own + relayed:
            @pl.when(cond)
            def _(shard=shard, slot=slot, target=target):
                remote(g, shard, slot, target).wait_send()
        return 0

    lax.fori_loop(0, groups, drain, 0)


def per_device(shards, queries, keys, values, doc_lengths):
    q, k, v = queries[0], keys[0], values[0]
    rows, heads, width = q.shape
    groups = k.shape[1]
    per_group = heads // groups
    docs = doc_lengths.shape[1]
    anywhere = pl.BlockSpec(memory_space=pl.ANY)
    out = pl.pallas_call(
        functools.partial(attention, docs),
        out_shape=jax.ShapeDtypeStruct(q.shape, jnp.bfloat16),
        in_specs=[pl.BlockSpec(memory_space=pltpu.SMEM), anywhere, anywhere, anywhere],
        out_specs=anywhere,
        scratch_shapes=[
            pltpu.VMEM((groups, rows, per_group, width), jnp.bfloat16),
            pltpu.VMEM((2, rows, groups, width), jnp.bfloat16),
            pltpu.VMEM((rows * groups, width), jnp.float32),
            pltpu.VMEM((groups, shards, 2, rows, width), jnp.bfloat16),
            pltpu.VMEM((groups, rows, per_group, width), jnp.bfloat16),
            pltpu.VMEM((rows * per_group, width), jnp.bfloat16),
            pltpu.VMEM((shards + 1, rows, width), jnp.bfloat16),
            pltpu.SemaphoreType.DMA((groups, 8)),
            pltpu.SemaphoreType.DMA((groups, shards)),
            pltpu.SemaphoreType.DMA((2 + groups,)),
            pltpu.SemaphoreType.DMA((groups,)),
        ],
        compiler_params=pltpu.CompilerParams(
            collective_id=0, has_side_effects=True, vmem_limit_bytes=60 * 1024 * 1024
        ),
        name="packed_attention",
    )(doc_lengths, q, k, v)
    return out[None]


def solution(mesh):
    placed = P("dp", "seq", None, None)
    return jax.shard_map(
        functools.partial(per_device, mesh.shape["seq"]),
        mesh=mesh,
        in_specs=(placed, placed, placed, P()),
        out_specs=placed,
        check_vma=False,
    )
```

```python
import functools

import jax
import jax.numpy as jnp
from jax import lax
from jax.experimental import pallas as pl
from jax.experimental.pallas import tpu as pltpu
from jax.sharding import PartitionSpec as P

MESH = pl.DeviceIdType.MESH
LOG2E = 1.4426950408889634
BIG = float(2.0**120)
AHEAD = 3


def attention(docs, lens, q_hbm, k_hbm, v_hbm, o_hbm, qv, raw, wide, kv, ov, q_mark, k_mark,
              score_a, score_b, weight_a, weight_b, send_sem, recv_sem, in_sem, out_sem):
    groups, shards, _, rows, width = kv.shape
    per_group = qv.shape[2]
    half = shards // 2
    dp = lax.axis_index("dp")
    me = lax.axis_index("seq")
    y = me % half
    upper = me >= half
    lower = me < half
    right = (y + 1) % half
    left = (y + half - 1) % half

    def q_copy(g):
        return pltpu.make_async_copy(
            q_hbm.at[:, pl.ds(pl.multiple_of(g * per_group, per_group), per_group), :], qv.at[g], in_sem.at[2 + g]
        )

    def o_copy(g):
        return pltpu.make_async_copy(
            ov.at[g], o_hbm.at[:, pl.ds(pl.multiple_of(g * per_group, per_group), per_group), :], out_sem.at[g]
        )

    k_in = pltpu.make_async_copy(k_hbm, raw.at[0], in_sem.at[0])
    v_in = pltpu.make_async_copy(v_hbm, raw.at[1], in_sem.at[1])
    k_in.start()
    v_in.start()
    for g in range(groups):
        q_copy(g).start()

    barrier = pltpu.get_barrier_semaphore()
    for step in range(1, shards):
        pl.semaphore_signal(barrier, inc=1, device_id=(dp, (me + step) % shards), device_id_type=MESH)

    for which, copy in ((0, k_in), (1, v_in)):
        copy.wait()
        wide[...] = raw[which].astype(jnp.float32).reshape(rows * groups, width)
        for g in range(groups):
            kv[g, me, which] = wide[pl.ds(g, rows, stride=groups), :].astype(jnp.bfloat16)

    pl.semaphore_wait(barrier, shards - 1)

    def remote(g, shard, slot, target, part=None):
        block = kv.at[g, shard] if part is None else kv.at[g, shard, part]
        return pltpu.make_async_remote_copy(
            src_ref=block,
            dst_ref=block,
            send_sem=send_sem.at[g, slot],
            recv_sem=recv_sem.at[g, shards if part == 1 else shard],
            device_id=(dp, target),
            device_id_type=MESH,
        )

    own = [
        (lower, me, 0, half + y, None),
        (lower, me, 1, right, None),
        (lower & (y < 2), me, 2, y + 2, None),
        (lower & (y < 1), me, 3, y + 3, None),
        (upper & (y < 3), me, 0, half + y + 1, None),
        (upper & (y == 0), me, 1, half + 3, None),
        (upper & (y == 1), me, 1, half + 3, 0),
    ]
    relayed = [
        (lower, left, 4, half + y, None),
        (upper, left, 2, half + right, None),
        (upper, y, 3, half + left, None),
        (upper & (y == 3), jnp.int32(half), 4, half + 2, None),
        (upper & (y == 2), jnp.int32(half + 1), 4, half + 3, 1),
    ]

    def start(table, g):
        for cond, shard, slot, target, part in table:
            @pl.when(cond)
            def _(shard=shard, slot=slot, target=target, part=part):
                remote(g, shard, slot, target, part).start()

    def arrived(g, shard, cond, part=None):
        @pl.when(cond)
        def _():
            remote(g, shard, 0, (me + 1) % shards, part).wait_recv()

    def relay(g):
        arrived(g, left, lower)
        arrived(g, left, upper)
        arrived(g, y, upper)
        arrived(g, jnp.int32(half), upper & (y == 3))
        arrived(g, jnp.int32(half + 1), upper & (y == 2))
        start(relayed, g)

    def rest(g):
        for s in range(shards - 1):
            if s < half:
                arrived(g, s, lower & (s < y - 1))
                arrived(g, s, upper & (s != y) & (s != left))
            elif s == half:
                arrived(g, s, upper & (s < me) & (y != 3))
            elif s == half + 1:
                arrived(g, s, me == shards - 1, 0)
                arrived(g, s, me == shards - 1, 1)
            else:
                arrived(g, s, s < me)

    for g in range(AHEAD):
        start(own, g)

    lane = lax.broadcasted_iota(jnp.int32, (1, width), 1)
    begin = jnp.zeros((1, width), jnp.int32)
    end = jnp.zeros((1, width), jnp.int32)
    so_far = jnp.int32(0)
    for j in range(docs):
        begin = jnp.where(lane == j, so_far, begin)
        so_far = so_far + lens[dp, j]
        end = jnp.where(lane == j, so_far, end)

    def mark_keys(s, _):
        place = s * rows + lax.broadcasted_iota(jnp.int32, (rows, width), 0)
        inside = (place >= begin) & (place < end)
        k_mark[s] = jnp.where(inside, 1.0, 0.0).astype(jnp.bfloat16)
        return 0

    lax.fori_loop(0, shards, mark_keys, 0)

    def mark_queries(s, _):
        spot = s * rows + lax.broadcasted_iota(jnp.int32, (rows, width), 0)
        place = me * rows + spot // per_group
        inside = ((place >= begin) & (place < end)) | (lane >= docs)
        q_mark[pl.ds(pl.multiple_of(s * rows, rows), rows), :] = jnp.where(inside, 0.0, -BIG).astype(jnp.bfloat16)
        return 0

    lax.fori_loop(0, per_group, mark_queries, 0)

    scale = float(width) ** -0.5 * LOG2E
    tile_tokens = 64
    tile = tile_tokens * per_group
    ones = jnp.ones((rows, width), jnp.bfloat16)

    def score_pass(g, t, count, score):
        q = qv[g, pl.ds(pl.multiple_of(t * tile_tokens, tile_tokens), tile_tokens)].reshape(tile, width)
        marks = q_mark[pl.ds(pl.multiple_of(t * tile, tile), tile), :]
        queries = jnp.concatenate([q, marks], axis=1)
        for s in range(count):
            k = jnp.concatenate([kv[g, s, 0], k_mark[s]], axis=1)
            part = lax.dot_general(queries, k, (((1,), (1,)), ((), ())), preferred_element_type=jnp.float32)
            if s == count - 1:
                token = t * tile_tokens + lax.broadcasted_iota(jnp.int32, (tile, rows), 0) // per_group
                column = lax.broadcasted_iota(jnp.int32, (tile, rows), 1)
                part = jnp.where(column <= token, part, -BIG)
            score[:, s * rows : (s + 1) * rows] = part

    def value_pass(g, t, count, score, weight):
        keys = count * rows
        top = jnp.max(score[:, :keys], axis=1, keepdims=True) * scale
        weight[:, :keys] = jnp.exp2(score[:, :keys] * scale - top).astype(jnp.bfloat16)
        v = jnp.concatenate(
            [jnp.concatenate([kv[g, s, 1], ones], axis=1) for s in range(count)], axis=0
        )
        summed = jnp.dot(weight[:, :keys], v, preferred_element_type=jnp.float32)
        out = (summed[:, :width] / summed[:, width:]).astype(jnp.bfloat16)
        ov[g, pl.ds(pl.multiple_of(t * tile_tokens, tile_tokens), tile_tokens)] = out.reshape(
            tile_tokens, per_group, width
        )

    def compute(g, t):
        for count in range(1, shards + 1):
            @pl.when(me == count - 1)
            def _(count=count):
                score_pass(g, t, count, score_a)
                score_pass(g, t + 1, count, score_b)
                value_pass(g, t, count, score_a, weight_a)
                value_pass(g, t + 1, count, score_b, weight_b)

    relay(0)
    relay(1)
    parts = rows // tile_tokens // 2

    def step(n, _):
        g = n // parts
        h = n % parts

        @pl.when(h == 0)
        def _():
            rest(g)
            q_copy(g).wait()

        @pl.when((h == 1) & (g + AHEAD < groups))
        def _():
            start(own, g + AHEAD)

        @pl.when((h == 1) & (g + 2 < groups))
        def _():
            relay(g + 2)

        compute(g, 2 * h)

        @pl.when(h == parts - 1)
        def _():
            o_copy(g).start()

        return 0

    lax.fori_loop(0, groups * parts, step, 0)

    def drain(g, _):
        o_copy(g).wait()
        for cond, shard, slot, target, part in own + relayed:
            @pl.when(cond)
            def _(shard=shard, slot=slot, target=target, part=part):
                remote(g, shard, slot, target, part).wait_send()
        return 0

    lax.fori_loop(0, groups, drain, 0)


def per_device(shards, queries, keys, values, doc_lengths):
    q, k, v = queries[0], keys[0], values[0]
    rows, heads, width = q.shape
    groups = k.shape[1]
    per_group = heads // groups
    docs = doc_lengths.shape[1]
    anywhere = pl.BlockSpec(memory_space=pl.ANY)
    out = pl.pallas_call(
        functools.partial(attention, docs),
        out_shape=jax.ShapeDtypeStruct(q.shape, jnp.bfloat16),
        in_specs=[pl.BlockSpec(memory_space=pltpu.SMEM), anywhere, anywhere, anywhere],
        out_specs=anywhere,
        scratch_shapes=[
            pltpu.VMEM((groups, rows, per_group, width), jnp.bfloat16),
            pltpu.VMEM((2, rows, groups, width), jnp.bfloat16),
            pltpu.VMEM((rows * groups, width), jnp.float32),
            pltpu.VMEM((groups, shards, 2, rows, width), jnp.bfloat16),
            pltpu.VMEM((groups, rows, per_group, width), jnp.bfloat16),
            pltpu.VMEM((rows * per_group, width), jnp.bfloat16),
            pltpu.VMEM((shards, rows, width), jnp.bfloat16),
            pltpu.VMEM((64 * per_group, shards * rows), jnp.float32),
            pltpu.VMEM((64 * per_group, shards * rows), jnp.float32),
            pltpu.VMEM((64 * per_group, shards * rows), jnp.bfloat16),
            pltpu.VMEM((64 * per_group, shards * rows), jnp.bfloat16),
            pltpu.SemaphoreType.DMA((groups, 5)),
            pltpu.SemaphoreType.DMA((groups, shards + 1)),
            pltpu.SemaphoreType.DMA((2 + groups,)),
            pltpu.SemaphoreType.DMA((groups,)),
        ],
        compiler_params=pltpu.CompilerParams(
            collective_id=0, has_side_effects=True, vmem_limit_bytes=60 * 1024 * 1024
        ),
        name="packed_attention",
    )(doc_lengths, q, k, v)
    return out[None]


def solution(mesh):
    placed = P("dp", "seq", None, None)
    return jax.shard_map(
        functools.partial(per_device, mesh.shape["seq"]),
        mesh=mesh,
        in_specs=(placed, placed, placed, P()),
        out_specs=placed,
        check_vma=False,
    )
```

```python
import functools

import jax
import jax.numpy as jnp
from jax import lax
from jax.experimental import pallas as pl
from jax.experimental.pallas import tpu as pltpu
from jax.sharding import PartitionSpec as P

MESH = pl.DeviceIdType.MESH
LOG2E = 1.4426950408889634
BIG = float(2.0**120)
READY = 2
SPREAD_HEAD = 1
TAIL_HEADS = 1


TILE_TOKENS = 64


def head_pass(me, g, t, qv, kv, ov, q_mark, k_mark, scores, weights):
    _, shards, _, rows, width = kv.shape
    per_group = qv.shape[2]
    scale = float(width) ** -0.5 * LOG2E
    tile = TILE_TOKENS * per_group

    def tokens(t):
        return pl.ds(pl.multiple_of(t * TILE_TOKENS, TILE_TOKENS), TILE_TOKENS)

    def score_pass(t, count, score):
        q = qv[g, tokens(t)].reshape(tile, width)
        marks = q_mark[pl.ds(pl.multiple_of(t * tile, tile), tile), :]
        queries = jnp.concatenate([q, marks], axis=1)
        for s in range(count):
            k = jnp.concatenate([kv[g, s, 0], k_mark[s]], axis=1)
            part = lax.dot_general(queries, k, (((1,), (1,)), ((), ())), preferred_element_type=jnp.float32)
            if s == count - 1:
                token = t * TILE_TOKENS + lax.broadcasted_iota(jnp.int32, (tile, rows), 0) // per_group
                column = lax.broadcasted_iota(jnp.int32, (tile, rows), 1)
                part = jnp.where(column <= token, part, -BIG)
            score[:, s * rows : (s + 1) * rows] = part

    def value_pass(t, count, score, weight):
        keys = count * rows
        top = jnp.max(score[:, :keys], axis=1, keepdims=True) * scale
        weight[:, :keys] = jnp.exp2(score[:, :keys] * scale - top).astype(jnp.bfloat16)
        ones = jnp.ones((rows, width), jnp.bfloat16)
        v = jnp.concatenate([jnp.concatenate([kv[g, s, 1], ones], axis=1) for s in range(count)], axis=0)
        summed = jnp.dot(weight[:, :keys], v, preferred_element_type=jnp.float32)
        out = (summed[:, :width] / summed[:, width:]).astype(jnp.bfloat16)
        ov[g, tokens(t)] = out.reshape(TILE_TOKENS, per_group, width)

    for count in range(1, shards + 1):
        @pl.when(me == count - 1)
        def _(count=count):
            for u in range(2):
                score_pass(t + u, count, scores.at[u])
            for u in range(2):
                value_pass(t + u, count, scores.at[u], weights.at[u])


def heads_of(ref, g, per_group, count=1):
    return ref.at[:, pl.ds(g * per_group, count * per_group), :]


def tail(part_hbm, q_hbm, kv_hbm, qm_hbm, km_hbm, o_hbm, qv, kv, ov, done, q_mark, k_mark, scores, weights,
         in_sem, kv_sem, out_sem):
    last, shards, _, rows, width = kv.shape
    per_group = qv.shape[2]
    first = done.shape[1] // per_group
    me = lax.axis_index("seq")
    marks = [pltpu.make_async_copy(km_hbm, k_mark, in_sem.at[0]), pltpu.make_async_copy(qm_hbm, q_mark, in_sem.at[1])]

    def q_copy(g):
        return pltpu.make_async_copy(heads_of(q_hbm, first + g, per_group), qv.at[g], in_sem.at[2 + g])

    def kv_copy(g, s):
        return pltpu.make_async_copy(kv_hbm.at[g, s], kv.at[g, s], kv_sem.at[g, s])

    def o_copy(g):
        return pltpu.make_async_copy(ov.at[g], heads_of(o_hbm, first + g, per_group), out_sem.at[g])

    done_in = pltpu.make_async_copy(heads_of(part_hbm, 0, per_group, first), done, in_sem.at[2 + last])
    done_out = pltpu.make_async_copy(done, heads_of(o_hbm, 0, per_group, first), out_sem.at[last])
    for copy in marks:
        copy.start()
    for g in range(last):
        q_copy(g).start()
        for s in range(shards):
            @pl.when(s <= me)
            def _(g=g, s=s):
                kv_copy(g, s).start()
    done_in.start()
    for copy in marks:
        copy.wait()
    parts = rows // TILE_TOKENS // 2

    def step(n, _):
        g = n // parts
        h = n % parts

        @pl.when(h == 0)
        def _():
            q_copy(g).wait()
            for s in range(shards):
                @pl.when(s <= me)
                def _(s=s):
                    kv_copy(g, s).wait()

        @pl.when(n == 1)
        def _():
            done_in.wait()
            done_out.start()

        head_pass(me, g, 2 * h, qv, kv, ov, q_mark, k_mark, scores, weights)

        @pl.when(h == parts - 1)
        def _():
            o_copy(g).start()

        return 0

    lax.fori_loop(0, last * parts, step, 0)
    for g in range(last):
        o_copy(g).wait()
    done_out.wait()


def attention(docs, lens, q_hbm, k_hbm, v_hbm, o_hbm, kv_hbm, qm_hbm, km_hbm, qv, raw, wide, kv, ov, q_mark, k_mark,
              scores, weights, send_sem, recv_sem, in_sem, out_sem, kv_sem):
    groups, shards, _, rows, width = kv.shape
    here = ov.shape[0]
    per_group = qv.shape[2]
    half = shards // 2
    dp = lax.axis_index("dp")
    me = lax.axis_index("seq")
    y = me % half
    upper = me >= half
    lower = me < half
    right = (y + 1) % half
    left = (y + half - 1) % half

    def q_copy(g):
        return pltpu.make_async_copy(heads_of(q_hbm, g, per_group), qv.at[g], in_sem.at[2 + g])

    def o_copy(g):
        return pltpu.make_async_copy(ov.at[g], heads_of(o_hbm, g, per_group), out_sem.at[g])

    def kv_copy(g, s):
        return pltpu.make_async_copy(kv.at[g, s], kv_hbm.at[g - here, s], kv_sem.at[g - here, s])

    k_in = pltpu.make_async_copy(k_hbm, raw.at[0], in_sem.at[0])
    v_in = pltpu.make_async_copy(v_hbm, raw.at[1], in_sem.at[1])
    k_in.start()
    v_in.start()
    for g in range(here):
        q_copy(g).start()

    barrier = pltpu.get_barrier_semaphore()
    for step in range(1, shards):
        pl.semaphore_signal(barrier, inc=1, device_id=(dp, (me + step) % shards), device_id_type=MESH)

    def own_block(g):
        for which in range(2):
            kv[g, me, which] = wide[which, pl.ds(g, rows, stride=groups), :].astype(jnp.bfloat16)

    for which, copy in ((0, k_in), (1, v_in)):
        copy.wait()
        wide[which] = raw[which].astype(jnp.float32).reshape(rows * groups, width)
    for g in range(READY):
        own_block(g)

    pl.semaphore_wait(barrier, shards - 1)

    def remote(g, shard, slot, target, part=None):
        block = kv.at[g, shard] if part is None else kv.at[g, shard, part]
        return pltpu.make_async_remote_copy(
            src_ref=block,
            dst_ref=block,
            send_sem=send_sem.at[g, slot],
            recv_sem=recv_sem.at[g, shards if part == 1 else shard],
            device_id=(dp, target),
            device_id_type=MESH,
        )

    def spread(g):
        return g == SPREAD_HEAD

    def otherwise(g):
        return jnp.logical_not(spread(g))

    def cross(g):
        return [], [(lower, me, 0, half + y, None)]

    def lower_ring(g):
        return [], [
            (lower, me, 1, right, None),
            (lower & (y < 2), me, 2, y + 2, None),
            (lower & (y < 1), me, 3, y + 3, None),
        ]

    def cross_left(g):
        waits = [(lower, left), (lower & (y == 3) & spread(g), jnp.int32(1))]
        return waits, [
            (lower, left, 4, half + y, None),
            (lower & (y == 3) & spread(g), jnp.int32(1), 3, half + 3, None),
        ]

    def upper_ring_relayed(g):
        return [], [
            (upper & (y == 0), me, 1, half + 3, None),
            (upper & (y == 1), me, 0, half + 2, None),
        ]

    def upper_ring(g):
        return [], [
            (upper & (y == 0), me, 0, half + 1, None),
            (upper & (y == 2), me, 0, half + 3, None),
            (upper & (y == 1) & otherwise(g), me, 1, half + 3, 0),
        ]

    def pass_right(g):
        return [(upper, left)], [(upper & ((y != 2) | otherwise(g)), left, 2, half + right, None)]

    def pass_left(g):
        return [(upper, y)], [(upper, y, 3, half + left, None)]

    def pass_upper(g):
        waits = [(upper & (y == 3), jnp.int32(half)), (upper & (y == 2), jnp.int32(half + 1))]
        return waits, [
            (upper & (y == 3), jnp.int32(half), 4, half + 2, None),
            (upper & (y == 2) & otherwise(g), jnp.int32(half + 1), 4, half + 3, 1),
            (upper & (y == 2) & spread(g), jnp.int32(half + 1), 4, half + 3, None),
        ]

    plan = [
        (upper_ring_relayed, 6), (pass_right, 2), (upper_ring, 8), (pass_upper, 2), (pass_left, 3),
        (cross_left, 4), (lower_ring, 8), (cross, 5),
    ]

    def arrived(g, shard, cond, part=None):
        @pl.when(cond)
        def _():
            remote(g, shard, 0, (me + 1) % shards, part).wait_recv()

    def serve(what, g):
        waits, copies = what(g)
        for cond, shard in waits:
            arrived(g, shard, cond)
        for cond, shard, slot, target, part in copies:
            @pl.when(cond)
            def _(shard=shard, slot=slot, target=target, part=part):
                remote(g, shard, slot, target, part).start()

    def serve_later(g, odd):
        for what, ahead in plan:
            if ahead % 2 == odd:
                later = g + (ahead + odd) // 2

                @pl.when(later < groups)
                def _(what=what, later=later):
                    serve(what, later)

    def rest(g):
        for s in range(shards - 1):
            if s < half:
                early = (y == 3) & spread(g) if s == 1 else False
                arrived(g, s, lower & (s < y - 1) & jnp.logical_not(early))
                arrived(g, s, upper & (s != y) & (s != left))
            elif s == half:
                arrived(g, s, upper & (s < me) & (y != 3))
            elif s == half + 1:
                last = me == shards - 1
                arrived(g, s, last & spread(g))
                arrived(g, s, last & otherwise(g), 0)
                arrived(g, s, last & otherwise(g), 1)
            else:
                arrived(g, s, s < me)

    opening = sorted(
        ((2 * g - ahead, place, what, g) for place, (what, ahead) in enumerate(plan) for g in range(groups) if 2 * g < ahead),
        key=lambda item: item[:2],
    )
    sends = [(what, g) for _, _, what, g in opening if not what(g)[0] and g < READY]
    for what, g in sends:
        serve(what, g)
    for g in range(READY, groups):
        own_block(g)

    lane = lax.broadcasted_iota(jnp.int32, (1, width), 1)
    begin = jnp.zeros((1, width), jnp.int32)
    end = jnp.zeros((1, width), jnp.int32)
    so_far = jnp.int32(0)
    for j in range(docs):
        begin = jnp.where(lane == j, so_far, begin)
        so_far = so_far + lens[dp, j]
        end = jnp.where(lane == j, so_far, end)

    def mark_keys(s, _):
        place = s * rows + lax.broadcasted_iota(jnp.int32, (rows, width), 0)
        inside = (place >= begin) & (place < end)
        k_mark[s] = jnp.where(inside, 1.0, 0.0).astype(jnp.bfloat16)
        return 0

    lax.fori_loop(0, shards, mark_keys, 0)

    def mark_queries(s, _):
        spot = s * rows + lax.broadcasted_iota(jnp.int32, (rows, width), 0)
        place = me * rows + spot // per_group
        inside = ((place >= begin) & (place < end)) | (lane >= docs)
        q_mark[pl.ds(pl.multiple_of(s * rows, rows), rows), :] = jnp.where(inside, 0.0, -BIG).astype(jnp.bfloat16)
        return 0

    lax.fori_loop(0, per_group, mark_queries, 0)
    marks = [pltpu.make_async_copy(k_mark, km_hbm, out_sem.at[here]), pltpu.make_async_copy(q_mark, qm_hbm, out_sem.at[here + 1])]
    for copy in marks:
        copy.start()

    for _, _, what, g in opening:
        if (what, g) not in sends:
            serve(what, g)
    parts = rows // TILE_TOKENS // 2

    def step(n, _):
        g = n // parts
        h = n % parts

        @pl.when(h == 0)
        def _():
            serve_later(g, 0)
            rest(g)

        @pl.when((h == 0) & (g < here))
        def _():
            q_copy(g).wait()

        @pl.when((h == 0) & (g >= here))
        def _():
            for s in range(shards):
                @pl.when(s <= me)
                def _(s=s):
                    kv_copy(g, s).start()

        @pl.when(h == 1)
        def _():
            serve_later(g, 1)

        @pl.when(g < here)
        def _():
            head_pass(me, g, 2 * h, qv, kv, ov, q_mark, k_mark, scores, weights)

        @pl.when((h == parts - 1) & (g < here))
        def _():
            o_copy(g).start()

        return 0

    lax.fori_loop(0, groups * parts, step, 0)
    for copy in marks:
        copy.wait()

    def drain(g, _):
        @pl.when(g < here)
        def _():
            o_copy(g).wait()

        @pl.when(g >= here)
        def _():
            for s in range(shards):
                @pl.when(s <= me)
                def _(s=s):
                    kv_copy(g, s).wait()

        for what, _ in plan:
            for cond, shard, slot, target, part in what(g)[1]:
                @pl.when(cond)
                def _(shard=shard, slot=slot, target=target, part=part):
                    remote(g, shard, slot, target, part).wait_send()
        return 0

    lax.fori_loop(0, groups, drain, 0)


def per_device(shards, queries, keys, values, doc_lengths):
    q, k, v = queries[0], keys[0], values[0]
    rows, heads, width = q.shape
    groups = k.shape[1]
    per_group = heads // groups
    docs = doc_lengths.shape[1]
    here = groups - TAIL_HEADS
    anywhere = pl.BlockSpec(memory_space=pl.ANY)
    tile = TILE_TOKENS * per_group
    bf16 = jnp.bfloat16
    working = [
        pltpu.VMEM((rows * per_group, width), bf16),
        pltpu.VMEM((shards, rows, width), bf16),
        pltpu.VMEM((2, tile, shards * rows), jnp.float32),
        pltpu.VMEM((2, tile, shards * rows), bf16),
    ]
    part, kv_last, q_mark, k_mark = pl.pallas_call(
        functools.partial(attention, docs),
        out_shape=[
            jax.ShapeDtypeStruct(q.shape, bf16),
            jax.ShapeDtypeStruct((TAIL_HEADS, shards, 2, rows, width), bf16),
            jax.ShapeDtypeStruct((rows * per_group, width), bf16),
            jax.ShapeDtypeStruct((shards, rows, width), bf16),
        ],
        in_specs=[pl.BlockSpec(memory_space=pltpu.SMEM), anywhere, anywhere, anywhere],
        out_specs=[anywhere] * 4,
        scratch_shapes=[
            pltpu.VMEM((here, rows, per_group, width), bf16),
            pltpu.VMEM((2, rows, groups, width), bf16),
            pltpu.VMEM((2, rows * groups, width), jnp.float32),
            pltpu.VMEM((groups, shards, 2, rows, width), bf16),
            pltpu.VMEM((here, rows, per_group, width), bf16),
            *working,
            pltpu.SemaphoreType.DMA((groups, 5)),
            pltpu.SemaphoreType.DMA((groups, shards + 1)),
            pltpu.SemaphoreType.DMA((2 + here,)),
            pltpu.SemaphoreType.DMA((here + 2,)),
            pltpu.SemaphoreType.DMA((TAIL_HEADS, shards)),
        ],
        compiler_params=pltpu.CompilerParams(
            collective_id=0, has_side_effects=True, vmem_limit_bytes=60 * 1024 * 1024
        ),
        name="packed_attention",
    )(doc_lengths, q, k, v)
    out = pl.pallas_call(
        tail,
        out_shape=jax.ShapeDtypeStruct(q.shape, bf16),
        in_specs=[anywhere] * 5,
        out_specs=anywhere,
        scratch_shapes=[
            pltpu.VMEM((TAIL_HEADS, rows, per_group, width), bf16),
            pltpu.VMEM((TAIL_HEADS, shards, 2, rows, width), bf16),
            pltpu.VMEM((TAIL_HEADS, rows, per_group, width), bf16),
            pltpu.VMEM((rows, here * per_group, width), bf16),
            *working,
            pltpu.SemaphoreType.DMA((3 + TAIL_HEADS,)),
            pltpu.SemaphoreType.DMA((TAIL_HEADS, shards)),
            pltpu.SemaphoreType.DMA((TAIL_HEADS + 1,)),
        ],
        compiler_params=pltpu.CompilerParams(vmem_limit_bytes=60 * 1024 * 1024),
        name="tail_attention",
    )(part, q, kv_last, q_mark, k_mark)
    return out[None]


def solution(mesh):
    placed = P("dp", "seq", None, None)
    return jax.shard_map(
        functools.partial(per_device, mesh.shape["seq"]),
        mesh=mesh,
        in_specs=(placed, placed, placed, P()),
        out_specs=placed,
        check_vma=False,
    )
```

```python
import functools

import jax
import jax.numpy as jnp
from jax import lax
from jax.experimental import pallas as pl
from jax.experimental.pallas import tpu as pltpu
from jax.sharding import PartitionSpec as P

MESH = pl.DeviceIdType.MESH
LOG2E = 1.4426950408889634
BIG = float(2.0**120)
READY = 2
SPREAD_HEAD = 1
TAIL_HEADS = 1


TILE_TOKENS = 64


def head_pass(me, g, t, qv, kv, ov, q_mark, k_mark, scores, weights):
    _, shards, _, rows, width = kv.shape
    per_group = qv.shape[2]
    scale = float(width) ** -0.5 * LOG2E
    tile = TILE_TOKENS * per_group

    def tokens(t):
        return pl.ds(pl.multiple_of(t * TILE_TOKENS, TILE_TOKENS), TILE_TOKENS)

    def score_pass(t, count, score):
        q = qv[g, tokens(t)].reshape(tile, width)
        marks = q_mark[pl.ds(pl.multiple_of(t * tile, tile), tile), :]
        queries = jnp.concatenate([q, marks], axis=1)
        for s in range(count):
            k = jnp.concatenate([kv[g, s, 0], k_mark[s]], axis=1)
            part = lax.dot_general(queries, k, (((1,), (1,)), ((), ())), preferred_element_type=jnp.float32)
            if s == count - 1:
                token = t * TILE_TOKENS + lax.broadcasted_iota(jnp.int32, (tile, rows), 0) // per_group
                column = lax.broadcasted_iota(jnp.int32, (tile, rows), 1)
                part = jnp.where(column <= token, part, -BIG)
            score[:, s * rows : (s + 1) * rows] = part

    def value_pass(t, count, score, weight):
        keys = count * rows
        top = jnp.max(score[:, :keys], axis=1, keepdims=True) * scale
        weight[:, :keys] = jnp.exp2(score[:, :keys] * scale - top).astype(jnp.bfloat16)
        ones = jnp.ones((rows, width), jnp.bfloat16)
        v = jnp.concatenate([jnp.concatenate([kv[g, s, 1], ones], axis=1) for s in range(count)], axis=0)
        summed = jnp.dot(weight[:, :keys], v, preferred_element_type=jnp.float32)
        out = (summed[:, :width] / summed[:, width:]).astype(jnp.bfloat16)
        ov[g, tokens(t)] = out.reshape(TILE_TOKENS, per_group, width)

    for count in range(1, shards + 1):
        @pl.when(me == count - 1)
        def _(count=count):
            for u in range(2):
                score_pass(t + u, count, scores.at[u])
            for u in range(2):
                value_pass(t + u, count, scores.at[u], weights.at[u])


def heads_of(ref, g, per_group, count=1):
    return ref.at[:, pl.ds(g * per_group, count * per_group), :]


def tail(part_hbm, q_hbm, kv_hbm, qm_hbm, km_hbm, o_hbm, qv, kv, ov, done, q_mark, k_mark, scores, weights,
         in_sem, kv_sem, out_sem):
    last, shards, _, rows, width = kv.shape
    per_group = qv.shape[2]
    first = done.shape[1] // per_group
    me = lax.axis_index("seq")
    marks = [pltpu.make_async_copy(km_hbm, k_mark, in_sem.at[0]), pltpu.make_async_copy(qm_hbm, q_mark, in_sem.at[1])]

    def q_copy(g):
        return pltpu.make_async_copy(heads_of(q_hbm, first + g, per_group), qv.at[g], in_sem.at[2 + g])

    def kv_copy(g, s):
        return pltpu.make_async_copy(kv_hbm.at[g, s], kv.at[g, s], kv_sem.at[g, s])

    parts = rows // TILE_TOKENS // 2

    def o_copy(g, h):
        some = pl.ds(h * (rows // parts), rows // parts)
        return pltpu.make_async_copy(
            ov.at[g, some], o_hbm.at[some, pl.ds((first + g) * per_group, per_group), :], out_sem.at[g * parts + h]
        )

    done_in = pltpu.make_async_copy(heads_of(part_hbm, 0, per_group, first), done, in_sem.at[2 + last])
    done_out = pltpu.make_async_copy(done, heads_of(o_hbm, 0, per_group, first), out_sem.at[last * parts])
    for copy in marks:
        copy.start()
    for g in range(last):
        q_copy(g).start()
        for s in range(shards):
            @pl.when(s <= me)
            def _(g=g, s=s):
                kv_copy(g, s).start()
    done_in.start()
    for copy in marks:
        copy.wait()

    def step(n, _):
        g = n // parts
        h = n % parts

        @pl.when(h == 0)
        def _():
            q_copy(g).wait()
            for s in range(shards):
                @pl.when(s <= me)
                def _(s=s):
                    kv_copy(g, s).wait()

        @pl.when(n == 1)
        def _():
            done_in.wait()
            done_out.start()

        head_pass(me, g, 2 * h, qv, kv, ov, q_mark, k_mark, scores, weights)

        o_copy(g, h).start()
        return 0

    lax.fori_loop(0, last * parts, step, 0)
    for g in range(last):
        for h in range(parts):
            o_copy(g, h).wait()
    done_out.wait()


def attention(docs, lens, q_hbm, k_hbm, v_hbm, o_hbm, kv_hbm, qm_hbm, km_hbm, qv, raw, wide, kv, ov, q_mark, k_mark,
              scores, weights, send_sem, recv_sem, in_sem, out_sem, kv_sem):
    groups, shards, _, rows, width = kv.shape
    here = ov.shape[0]
    per_group = qv.shape[2]
    half = shards // 2
    dp = lax.axis_index("dp")
    me = lax.axis_index("seq")
    y = me % half
    upper = me >= half
    lower = me < half
    right = (y + 1) % half
    left = (y + half - 1) % half

    def q_copy(g):
        return pltpu.make_async_copy(heads_of(q_hbm, g, per_group), qv.at[g], in_sem.at[2 + g])

    def o_copy(g):
        return pltpu.make_async_copy(ov.at[g], heads_of(o_hbm, g, per_group), out_sem.at[g])

    def kv_copy(g, s):
        return pltpu.make_async_copy(kv.at[g, s], kv_hbm.at[g - here, s], kv_sem.at[g - here, s])

    k_in = pltpu.make_async_copy(k_hbm, raw.at[0], in_sem.at[0])
    v_in = pltpu.make_async_copy(v_hbm, raw.at[1], in_sem.at[1])
    k_in.start()
    v_in.start()
    for g in range(here):
        q_copy(g).start()

    barrier = pltpu.get_barrier_semaphore()
    for step in range(1, shards):
        pl.semaphore_signal(barrier, inc=1, device_id=(dp, (me + step) % shards), device_id_type=MESH)

    def own_block(g):
        for which in range(2):
            kv[g, me, which] = wide[which, pl.ds(g, rows, stride=groups), :].astype(jnp.bfloat16)

    for which, copy in ((0, k_in), (1, v_in)):
        copy.wait()
        wide[which] = raw[which].astype(jnp.float32).reshape(rows * groups, width)
    for g in range(READY):
        own_block(g)

    pl.semaphore_wait(barrier, shards - 1)

    def remote(g, shard, slot, target, part=None):
        block = kv.at[g, shard] if part is None else kv.at[g, shard, part]
        return pltpu.make_async_remote_copy(
            src_ref=block,
            dst_ref=block,
            send_sem=send_sem.at[g, slot],
            recv_sem=recv_sem.at[g, shards if part == 1 else shard],
            device_id=(dp, target),
            device_id_type=MESH,
        )

    def spread(g):
        return g == SPREAD_HEAD

    def otherwise(g):
        return jnp.logical_not(spread(g))

    def cross(g):
        return [], [(lower, me, 0, half + y, None)]

    def lower_ring(g):
        return [], [
            (lower, me, 1, right, None),
            (lower & (y < 2), me, 2, y + 2, None),
            (lower & (y < 1), me, 3, y + 3, None),
        ]

    def cross_left(g):
        waits = [(lower, left), (lower & (y == 3) & spread(g), jnp.int32(1))]
        return waits, [
            (lower, left, 4, half + y, None),
            (lower & (y == 3) & spread(g), jnp.int32(1), 3, half + 3, None),
        ]

    def upper_ring_relayed(g):
        return [], [
            (upper & (y == 0), me, 1, half + 3, None),
            (upper & (y == 1), me, 0, half + 2, None),
        ]

    def upper_ring(g):
        return [], [
            (upper & (y == 0), me, 0, half + 1, None),
            (upper & (y == 2), me, 0, half + 3, None),
            (upper & (y == 1) & otherwise(g), me, 1, half + 3, 0),
        ]

    def pass_right(g):
        return [(upper, left)], [(upper & ((y != 2) | otherwise(g)), left, 2, half + right, None)]

    def pass_left(g):
        return [(upper, y)], [(upper, y, 3, half + left, None)]

    def pass_upper(g):
        waits = [(upper & (y == 3), jnp.int32(half)), (upper & (y == 2), jnp.int32(half + 1))]
        return waits, [
            (upper & (y == 3), jnp.int32(half), 4, half + 2, None),
            (upper & (y == 2) & otherwise(g), jnp.int32(half + 1), 4, half + 3, 1),
            (upper & (y == 2) & spread(g), jnp.int32(half + 1), 4, half + 3, None),
        ]

    plan = [
        (upper_ring_relayed, 6), (pass_right, 2), (upper_ring, 8), (pass_upper, 2), (pass_left, 3),
        (cross_left, 4), (lower_ring, 8), (cross, 5),
    ]

    def arrived(g, shard, cond, part=None):
        @pl.when(cond)
        def _():
            remote(g, shard, 0, (me + 1) % shards, part).wait_recv()

    def serve(what, g):
        waits, copies = what(g)
        for cond, shard in waits:
            arrived(g, shard, cond)
        for cond, shard, slot, target, part in copies:
            @pl.when(cond)
            def _(shard=shard, slot=slot, target=target, part=part):
                remote(g, shard, slot, target, part).start()

    def serve_later(g, odd):
        for what, ahead in plan:
            if ahead % 2 == odd:
                later = g + (ahead + odd) // 2

                @pl.when(later < groups)
                def _(what=what, later=later):
                    serve(what, later)

    def rest(g):
        for s in range(shards - 1):
            if s < half:
                early = (y == 3) & spread(g) if s == 1 else False
                arrived(g, s, lower & (s < y - 1) & jnp.logical_not(early))
                arrived(g, s, upper & (s != y) & (s != left))
            elif s == half:
                arrived(g, s, upper & (s < me) & (y != 3))
            elif s == half + 1:
                last = me == shards - 1
                arrived(g, s, last & spread(g))
                arrived(g, s, last & otherwise(g), 0)
                arrived(g, s, last & otherwise(g), 1)
            else:
                arrived(g, s, s < me)

    opening = sorted(
        ((2 * g - ahead, place, what, g) for place, (what, ahead) in enumerate(plan) for g in range(groups) if 2 * g < ahead),
        key=lambda item: item[:2],
    )
    sends = [(what, g) for _, _, what, g in opening if not what(g)[0] and g < READY]
    for what, g in sends:
        serve(what, g)
    for g in range(READY, groups):
        own_block(g)

    lane = lax.broadcasted_iota(jnp.int32, (1, width), 1)
    begin = jnp.zeros((1, width), jnp.int32)
    end = jnp.zeros((1, width), jnp.int32)
    so_far = jnp.int32(0)
    for j in range(docs):
        begin = jnp.where(lane == j, so_far, begin)
        so_far = so_far + lens[dp, j]
        end = jnp.where(lane == j, so_far, end)

    def mark_keys(s, _):
        place = s * rows + lax.broadcasted_iota(jnp.int32, (rows, width), 0)
        inside = (place >= begin) & (place < end)
        k_mark[s] = jnp.where(inside, 1.0, 0.0).astype(jnp.bfloat16)
        return 0

    lax.fori_loop(0, shards, mark_keys, 0)

    def mark_queries(s, _):
        spot = s * rows + lax.broadcasted_iota(jnp.int32, (rows, width), 0)
        place = me * rows + spot // per_group
        inside = ((place >= begin) & (place < end)) | (lane >= docs)
        q_mark[pl.ds(pl.multiple_of(s * rows, rows), rows), :] = jnp.where(inside, 0.0, -BIG).astype(jnp.bfloat16)
        return 0

    lax.fori_loop(0, per_group, mark_queries, 0)
    marks = [pltpu.make_async_copy(k_mark, km_hbm, out_sem.at[here]), pltpu.make_async_copy(q_mark, qm_hbm, out_sem.at[here + 1])]
    for copy in marks:
        copy.start()

    for _, _, what, g in opening:
        if (what, g) not in sends:
            serve(what, g)
    parts = rows // TILE_TOKENS // 2

    def keep(g, early):
        for s in range(shards):
            known = (s == me) | (upper & ((s == y) | (s == left)))
            wanted = known if early else jnp.logical_not(known)

            @pl.when((g >= here) & (s <= me) & wanted)
            def _(s=s):
                kv_copy(g, s).start()

    def step(n, _):
        g = n // parts
        h = n % parts

        @pl.when(h == 0)
        def _():
            serve_later(g, 0)
            keep(g, True)
            rest(g)

        @pl.when((h == 0) & (g < here))
        def _():
            q_copy(g).wait()

        @pl.when((h == 0) & (g >= here))
        def _():
            keep(g, False)

        @pl.when(h == 1)
        def _():
            serve_later(g, 1)

        @pl.when(g < here)
        def _():
            head_pass(me, g, 2 * h, qv, kv, ov, q_mark, k_mark, scores, weights)

        @pl.when((h == parts - 1) & (g < here))
        def _():
            o_copy(g).start()

        return 0

    lax.fori_loop(0, groups * parts, step, 0)
    for copy in marks:
        copy.wait()

    def drain(g, _):
        @pl.when(g < here)
        def _():
            o_copy(g).wait()

        @pl.when(g >= here)
        def _():
            for s in range(shards):
                @pl.when(s <= me)
                def _(s=s):
                    kv_copy(g, s).wait()

        for what, _ in plan:
            for cond, shard, slot, target, part in what(g)[1]:
                @pl.when(cond)
                def _(shard=shard, slot=slot, target=target, part=part):
                    remote(g, shard, slot, target, part).wait_send()
        return 0

    lax.fori_loop(0, groups, drain, 0)


def per_device(shards, queries, keys, values, doc_lengths):
    q, k, v = queries[0], keys[0], values[0]
    rows, heads, width = q.shape
    groups = k.shape[1]
    per_group = heads // groups
    docs = doc_lengths.shape[1]
    here = groups - TAIL_HEADS
    anywhere = pl.BlockSpec(memory_space=pl.ANY)
    tile = TILE_TOKENS * per_group
    bf16 = jnp.bfloat16
    working = [
        pltpu.VMEM((rows * per_group, width), bf16),
        pltpu.VMEM((shards, rows, width), bf16),
        pltpu.VMEM((2, tile, shards * rows), jnp.float32),
        pltpu.VMEM((2, tile, shards * rows), bf16),
    ]
    part, kv_last, q_mark, k_mark = pl.pallas_call(
        functools.partial(attention, docs),
        out_shape=[
            jax.ShapeDtypeStruct(q.shape, bf16),
            jax.ShapeDtypeStruct((TAIL_HEADS, shards, 2, rows, width), bf16),
            jax.ShapeDtypeStruct((rows * per_group, width), bf16),
            jax.ShapeDtypeStruct((shards, rows, width), bf16),
        ],
        in_specs=[pl.BlockSpec(memory_space=pltpu.SMEM), anywhere, anywhere, anywhere],
        out_specs=[anywhere] * 4,
        scratch_shapes=[
            pltpu.VMEM((here, rows, per_group, width), bf16),
            pltpu.VMEM((2, rows, groups, width), bf16),
            pltpu.VMEM((2, rows * groups, width), jnp.float32),
            pltpu.VMEM((groups, shards, 2, rows, width), bf16),
            pltpu.VMEM((here, rows, per_group, width), bf16),
            *working,
            pltpu.SemaphoreType.DMA((groups, 5)),
            pltpu.SemaphoreType.DMA((groups, shards + 1)),
            pltpu.SemaphoreType.DMA((2 + here,)),
            pltpu.SemaphoreType.DMA((here + 2,)),
            pltpu.SemaphoreType.DMA((TAIL_HEADS, shards)),
        ],
        compiler_params=pltpu.CompilerParams(
            collective_id=0, has_side_effects=True, vmem_limit_bytes=60 * 1024 * 1024
        ),
        name="packed_attention",
    )(doc_lengths, q, k, v)
    out = pl.pallas_call(
        tail,
        out_shape=jax.ShapeDtypeStruct(q.shape, bf16),
        in_specs=[anywhere] * 5,
        out_specs=anywhere,
        scratch_shapes=[
            pltpu.VMEM((TAIL_HEADS, rows, per_group, width), bf16),
            pltpu.VMEM((TAIL_HEADS, shards, 2, rows, width), bf16),
            pltpu.VMEM((TAIL_HEADS, rows, per_group, width), bf16),
            pltpu.VMEM((rows, here * per_group, width), bf16),
            *working,
            pltpu.SemaphoreType.DMA((3 + TAIL_HEADS,)),
            pltpu.SemaphoreType.DMA((TAIL_HEADS, shards)),
            pltpu.SemaphoreType.DMA((TAIL_HEADS * (rows // TILE_TOKENS // 2) + 1,)),
        ],
        compiler_params=pltpu.CompilerParams(vmem_limit_bytes=60 * 1024 * 1024),
        name="tail_attention",
    )(part, q, kv_last, q_mark, k_mark)
    return out[None]


def solution(mesh):
    placed = P("dp", "seq", None, None)
    return jax.shard_map(
        functools.partial(per_device, mesh.shape["seq"]),
        mesh=mesh,
        in_specs=(placed, placed, placed, P()),
        out_specs=placed,
        check_vma=False,
    )
```
